32 devices in a mesh: ia: 4 (over z), ja: 4 (over y, core), ka: 2 (over x).
Axes of the slice: x: 2, y: 2, z: 4, core: 2. Of those that a mesh axis runs over, the one named last changes fastest.
Arguments:
- tensor: float32 [8192, 8, 1024], P('ja', 'ka', 'ia'), may hold values from -6 to 6
- factor_a: float32 [1024, 128], P('ia'), may hold values from -1 to 1
- factor_c: float32 [8, 128], P('ka'), may hold values from -2 to 2
- gram_c: float32 [128, 128], replicated, may hold values from -12 to 24, as said below
Outputs:
- factor_b: float32 [8192, 128], P('ja')
- factor_c_new: float32 [8, 128], P('ka')
The draws below stay inside these ranges and needn't reach their ends.
Inputs may be any that keep to these rules, and one draw needn't show every extreme that they name: `gram_c`: symmetric positive definite.
All inputs are finite; a program needn't handle non-finite values.
Results may differ from the reference program's by a relative error of at most 0.000071.
Values sent between devices are 32-bit elements; how exact they have to be, the bound alone decides.
A program may use at most 64 MiB of HBM per device.

```python
import jax
import jax.numpy as jnp
from jax import lax

R = 128
I = 1024
J = 8192
K = 8


def draw_factor_a(key, part):
    first, second, third = jax.random.split(jax.random.fold_in(key, 11), 3)
    noise = jnp.clip(jax.random.normal(first, (I, R), jnp.float32), -4.0, 4.0)
    common = jnp.clip(jax.random.normal(second, (I, 1), jnp.float32), -4.0, 4.0)
    weights = jnp.clip(jax.random.normal(third, (1, R), jnp.float32), -4.0, 4.0)
    return ((noise + 0.7 * common * weights) / jnp.sqrt(jnp.float32(I))).astype(jnp.float32)


def draw_gram_c(key, part):
    first, second = jax.random.split(jax.random.fold_in(key, 23), 2)
    mixing = jnp.clip(jax.random.normal(first, (R, R), jnp.float32), -4.0, 4.0)
    shared = jnp.clip(jax.random.normal(second, (R,), jnp.float32), -3.0, 3.0)
    result = 0.5 * jnp.eye(R, dtype=jnp.float32) + jnp.dot(mixing, mixing.T) / R + 0.3 * jnp.outer(shared, shared)
    return jnp.clip(result, -12.0, 24.0).astype(jnp.float32)


def block_scale(stream_key, extent, pieces, smallest, high):
    def one(axis_at, parts):
        steps = jax.random.uniform(jax.random.fold_in(jax.random.fold_in(stream_key, 6), axis_at), (parts,), jnp.float32, smallest / len(pieces), high / len(pieces))
        return jnp.repeat(jnp.exp(steps), extent[axis_at] // parts).reshape((-1,) + (1,) * (len(extent) - axis_at - 1))

    loudness = one(*pieces[0])
    for cut in pieces[1:]:
        loudness = loudness * one(*cut)
    return loudness


def bell_draw(rng, shape, scale, bound, cuts=(), kind=jnp.bfloat16):
    values = jax.random.normal(rng, shape, jnp.float32) * scale
    if len(cuts) > 0:
        values = block_scale(rng, shape, cuts, -0.22, 0.18) * values
    return jnp.clip(values, min=-bound, max=bound).astype(kind)


def setup_inputs(seed: int = 0) -> dict:
    arg_keys = jax.random.split(jax.random.key(seed), 5)
    tensor = bell_draw(arg_keys[0], (J, K, I), 1.0, 6.0, ((0, 4), (1, 2), (2, 4)), jnp.float32)
    factor_a = draw_factor_a(jax.random.fold_in(arg_keys[4], 71), 0)
    factor_c = bell_draw(arg_keys[2], (K, R), K ** -0.5, 2.0, ((0, 2),), jnp.float32)
    gram_c = draw_gram_c(jax.random.fold_in(arg_keys[4], 71), 0)
    return {"tensor": tensor, "factor_a": factor_a, "factor_c": factor_c, "gram_c": gram_c}


def right_solve(rhs, system):
    lower = jnp.linalg.cholesky(system)
    middle = lax.linalg.triangular_solve(lower, rhs, left_side=False, lower=True, transpose_a=True)
    return lax.linalg.triangular_solve(lower, middle, left_side=False, lower=True, transpose_a=False)

def reference(tensor, factor_a, factor_c, gram_c):
    high = lax.Precision.HIGHEST
    partial_value = jnp.dot(tensor.reshape(J * K, I).astype(jnp.float32), factor_a.astype(jnp.float32), precision=high, preferred_element_type=jnp.float32).reshape(J, K, R)
    gram_a = jnp.dot(factor_a.T.astype(jnp.float32), factor_a.astype(jnp.float32), precision=high, preferred_element_type=jnp.float32)
    mttkrp_b = jnp.sum(partial_value * factor_c[None, :, :], axis=1)
    factor_b = right_solve(mttkrp_b, gram_a * gram_c)
    mttkrp_c = jnp.sum(partial_value * factor_b[:, None, :], axis=0)
    gram_b = jnp.dot(factor_b.T.astype(jnp.float32), factor_b.astype(jnp.float32), precision=high, preferred_element_type=jnp.float32)
    factor_c_new = right_solve(mttkrp_c, gram_a * gram_b)
    return (factor_b, factor_c_new)
```

```python
import functools

import jax
import jax.numpy as jnp
from jax import lax
from jax.experimental import pallas as pl
from jax.experimental.pallas import tpu as pltpu
from jax.sharding import PartitionSpec as P

HIGH = lax.Precision.HIGHEST
MESH = pl.DeviceIdType.MESH
GROUP = 8


def mm(a, b):
    return jnp.dot(a, b, precision=HIGH, preferred_element_type=jnp.float32)


def mtm(a):
    return lax.dot_general(
        a, a, (((0,), (0,)), ((), ())), precision=HIGH, preferred_element_type=jnp.float32
    )


def eliminate(a):
    n = a.shape[0]
    lane = lax.broadcasted_iota(jnp.int32, (n, n), 1)
    sub = lax.broadcasted_iota(jnp.int32, (n, n), 0)
    lane_row = lax.broadcasted_iota(jnp.int32, (1, n), 1)
    for t in range(GROUP):
        col = jnp.broadcast_to(a[:, t : t + 1], (n, n))
        inv = 1.0 / col[t : t + 1, :]
        row = jnp.where(lane_row == t, inv, a[t : t + 1, :] * inv)
        a = jnp.where(sub == t, row, jnp.where(lane == t, 0.0, a) - col * row)
    a = pltpu.roll(a, n - GROUP, axis=1)
    return jnp.concatenate([a[GROUP:], a[:GROUP]], axis=0)


def kernel(
    dims,
    blocks,
    t_hbm,
    a_ref,
    c_ref,
    gc_ref,
    b_out,
    c_out,
    tbuf,
    part,
    mloc,
    xrecv,
    xsum,
    zrecv,
    bfull,
    ga_all,
    gb_all,
    mc_all,
    inv_ref,
    acc_ref,
    t_sem,
    x_send,
    x_recv,
    z_send,
    z_recv,
    p_send,
    p_recv,
    q_send,
    q_recv,
    ga_send,
    ga_recv,
    gb_send,
    gb_recv,
    mc_send,
    mc_recv,
    o_sem,
):
    ni, nj, nk = dims
    kl, rows, rank = part.shape
    jb = rows // blocks
    jx = jb // nk
    jz = jx // ni
    mi, mj, mk = lax.axis_index("ia"), lax.axis_index("ja"), lax.axis_index("ka")
    sends = []

    def peer(axis, me, n, d):
        return {axis: lax.rem(me + d, n)}

    def remote(src, dst, ss, rs, who):
        cp = pltpu.make_async_remote_copy(
            src_ref=src, dst_ref=dst, send_sem=ss, recv_sem=rs, device_id=who, device_id_type=MESH
        )
        cp.start()
        sends.append(cp)
        return cp

    tcopies = {}
    for b in range(blocks):
        for k in range(kl):
            rs = pl.ds(b * jb, jb)
            cp = pltpu.make_async_copy(t_hbm.at[rs, k, :], tbuf.at[k, rs, :], t_sem.at[b, k])
            cp.start()
            tcopies[b, k] = cp

    barrier = pltpu.get_barrier_semaphore()
    for axis, me, n in (("ia", mi, ni), ("ja", mj, nj), ("ka", mk, nk)):
        for d in range(1, n):
            pl.semaphore_signal(
                barrier, inc=1, device_id=peer(axis, me, n, d), device_id_type=MESH
            )

    a = a_ref[...]
    a_hi = a.astype(jnp.bfloat16)
    a_lo = (a - a_hi.astype(jnp.float32)).astype(jnp.bfloat16)
    weights = jnp.concatenate([a_hi, a_lo], axis=1)
    ga_all[mi] = mtm(a)
    pl.semaphore_wait(barrier, ni + nj + nk - 3)
    ga_cp = [
        remote(ga_all.at[mi], ga_all.at[mi], ga_send.at[d - 1], ga_recv.at[d - 1], peer("ia", mi, ni, d))
        for d in range(1, ni)
    ]

    x_cp, z_cp, p_cp, q_cp = {}, {}, {}, {}
    step = min(256, jb)

    def first(b):
        for k in range(kl):
            tcopies[b, k].wait()

        def chunk(s, carry):
            rs = pl.ds(pl.multiple_of(b * jb + s * step, step), step)
            total = None
            for k in range(kl):
                x = tbuf[k, rs, :]
                hi = x.astype(jnp.bfloat16)
                lo = (x - hi.astype(jnp.float32)).astype(jnp.bfloat16)
                y = jnp.dot(hi, weights, preferred_element_type=jnp.float32) + jnp.dot(
                    lo, weights, preferred_element_type=jnp.float32
                )
                y = y[:, :rank] + y[:, rank:]
                part[k, rs, :] = y
                y = y * c_ref[k : k + 1, :]
                total = y if total is None else total + y
            mloc[rs, :] = total
            return carry

        lax.fori_loop(0, jb // step, chunk, 0)
        for d in range(1, nk):
            other = lax.rem(mk + d, nk)
            rs = pl.ds(pl.multiple_of(b * jb + other * jx, 8), jx)
            x_cp[b, d] = remote(
                mloc.at[rs, :], xrecv.at[b, d - 1], x_send.at[b, d - 1], x_recv.at[b, d - 1],
                peer("ka", mk, nk, d),
            )

    def second(b):
        total = mloc[pl.ds(pl.multiple_of(b * jb + mk * jx, 8), jx), :]
        for d in range(1, nk):
            x_cp[b, d].wait_recv()
            total = total + xrecv[b, d - 1]
        xsum[b] = total
        for d in range(1, ni):
            other = lax.rem(mi + d, ni)
            z_cp[b, d] = remote(
                xsum.at[b, pl.ds(pl.multiple_of(other * jz, 8), jz), :], zrecv.at[b, d - 1],
                z_send.at[b, d - 1], z_recv.at[b, d - 1], peer("ia", mi, ni, d),
            )

    def third(b):
        total = xsum[b, pl.ds(pl.multiple_of(mi * jz, 8), jz), :]
        for d in range(1, ni):
            z_cp[b, d].wait_recv()
            total = total + zrecv[b, d - 1]
        rs = pl.ds(pl.multiple_of(b * jb + mk * jx + mi * jz, 8), jz)
        bfull[rs, :] = mm(total, inv_ref[...])
        for d in range(1, ni):
            p_cp[b, d] = remote(
                bfull.at[rs, :], bfull.at[rs, :], p_send.at[b, d - 1], p_recv.at[b, d - 1],
                peer("ia", mi, ni, d),
            )

    def fourth(b):
        for d in range(1, ni):
            p_cp[b, d].wait_recv()
        rs = pl.ds(pl.multiple_of(b * jb + mk * jx, 8), jx)
        for d in range(1, nk):
            q_cp[b, d] = remote(
                bfull.at[rs, :], bfull.at[rs, :], q_send.at[b, d - 1], q_recv.at[b, d - 1],
                peer("ka", mk, nk, d),
            )

    out_cp = []

    def fifth(b):
        for d in range(1, nk):
            q_cp[b, d].wait_recv()
        rs = pl.ds(b * jb, jb)
        cp = pltpu.make_async_copy(bfull.at[rs, :], b_out.at[rs, :], o_sem.at[b])
        cp.start()
        out_cp.append(cp)
        value = bfull[rs, :]
        acc_ref[pl.ds(0, rank), :] = acc_ref[pl.ds(0, rank), :] + mtm(value)
        for k in range(kl):
            s = jnp.sum(part[k, rs, :] * value, axis=0, keepdims=True)
            acc_ref[pl.ds(rank + k, 1), :] = acc_ref[pl.ds(rank + k, 1), :] + s

    for b in range(blocks):
        first(b)

    for cp in ga_cp:
        cp.wait_recv()
    gram_a = ga_all[0]
    for d in range(1, ni):
        gram_a = gram_a + ga_all[d]
    inv_ref[...] = gram_a * gc_ref[...]
    acc_ref[...] = jnp.zeros_like(acc_ref)
    groups = rank // GROUP
    for b in range(blocks):
        lo, hi = groups * b // blocks, groups * (b + 1) // blocks
        inv_ref[...] = lax.fori_loop(lo, hi, lambda _, v: eliminate(v), inv_ref[...])
        second(b)
    for b in range(blocks + 2):
        if b < blocks:
            third(b)
        if 1 <= b <= blocks:
            fourth(b - 1)
        if b >= 2:
            fifth(b - 2)

    gb_all[mj] = acc_ref[...]
    gb_cp = [
        remote(gb_all.at[mj], gb_all.at[mj], gb_send.at[d - 1], gb_recv.at[d - 1], peer("ja", mj, nj, d))
        for d in range(1, nj)
    ]
    for cp in gb_cp:
        cp.wait_recv()
    total = gb_all[0]
    for d in range(1, nj):
        total = total + gb_all[d]
    mc_all[mi] = total[rank:, :]
    mc_cp = [
        remote(mc_all.at[mi], mc_all.at[mi], mc_send.at[d - 1], mc_recv.at[d - 1], peer("ia", mi, ni, d))
        for d in range(1, ni)
    ]
    gram_a = ga_all[0]
    for d in range(1, ni):
        gram_a = gram_a + ga_all[d]
    inverse = lax.fori_loop(
        0, groups, lambda _, v: eliminate(v), gram_a * total[:rank, :]
    )
    for cp in mc_cp:
        cp.wait_recv()
    mttkrp_c = mc_all[0]
    for d in range(1, ni):
        mttkrp_c = mttkrp_c + mc_all[d]
    c_out[...] = mm(mttkrp_c, inverse)[:kl, :]
    for cp in out_cp:
        cp.wait()
    for cp in sends:
        cp.wait_send()


def body(dims, tensor, factor_a, factor_c, gram_c):
    ni, nj, nk = dims
    rows, kl, il = tensor.shape
    rank = factor_a.shape[1]
    blocks = 4
    jb = rows // blocks
    jx = jb // nk
    jz = jx // ni
    kp = -(-kl // 8) * 8
    f32 = jnp.float32
    dma = pltpu.SemaphoreType.DMA
    vmem = pl.BlockSpec(memory_space=pltpu.VMEM)
    return pl.pallas_call(
        functools.partial(kernel, dims, blocks),
        out_shape=(
            jax.ShapeDtypeStruct((rows, rank), f32),
            jax.ShapeDtypeStruct((kl, rank), f32),
        ),
        in_specs=[pl.BlockSpec(memory_space=pl.ANY), vmem, vmem, vmem],
        out_specs=(pl.BlockSpec(memory_space=pl.ANY), vmem),
        scratch_shapes=[
            pltpu.VMEM((kl, rows, il), f32),
            pltpu.VMEM((kl, rows, rank), f32),
            pltpu.VMEM((rows, rank), f32),
            pltpu.VMEM((blocks, nk - 1, jx, rank), f32),
            pltpu.VMEM((blocks, jx, rank), f32),
            pltpu.VMEM((blocks, ni - 1, jz, rank), f32),
            pltpu.VMEM((rows, rank), f32),
            pltpu.VMEM((ni, rank, rank), f32),
            pltpu.VMEM((nj, rank + kp, rank), f32),
            pltpu.VMEM((ni, kp, rank), f32),
            pltpu.VMEM((rank, rank), f32),
            pltpu.VMEM((rank + kp, rank), f32),
            dma((blocks, kl)),
            dma((blocks, nk - 1)),
            dma((blocks, nk - 1)),
            dma((blocks, ni - 1)),
            dma((blocks, ni - 1)),
            dma((blocks, ni - 1)),
            dma((blocks, ni - 1)),
            dma((blocks, nk - 1)),
            dma((blocks, nk - 1)),
            dma((ni - 1,)),
            dma((ni - 1,)),
            dma((nj - 1,)),
            dma((nj - 1,)),
            dma((ni - 1,)),
            dma((ni - 1,)),
            dma((blocks,)),
        ],
        compiler_params=pltpu.CompilerParams(
            collective_id=0, has_side_effects=True, vmem_limit_bytes=48 * 1024 * 1024
        ),
    )(tensor, factor_a, factor_c, gram_c)


def solution(mesh):
    dims = (mesh.shape["ia"], mesh.shape["ja"], mesh.shape["ka"])
    placed = (P("ja", "ka", "ia"), P("ia", None), P("ka", None), P())
    return jax.shard_map(
        functools.partial(body, dims),
        mesh=mesh,
        in_specs=placed,
        out_specs=(P("ja", None), P("ka", None)),
        check_vma=False,
    )
```

```python
import functools

import jax
import jax.numpy as jnp
from jax import lax
from jax.experimental import pallas as pl
from jax.experimental.pallas import tpu as pltpu
from jax.sharding import PartitionSpec as P

HIGH = lax.Precision.HIGHEST
MESH = pl.DeviceIdType.MESH
GROUP = 8


def mm(a, b):
    return jnp.dot(a, b, precision=HIGH, preferred_element_type=jnp.float32)


def mtm(a):
    return lax.dot_general(
        a, a, (((0,), (0,)), ((), ())), precision=HIGH, preferred_element_type=jnp.float32
    )


def eliminate(a):
    n = a.shape[0]
    lane = lax.broadcasted_iota(jnp.int32, (n, n), 1)
    sub = lax.broadcasted_iota(jnp.int32, (n, n), 0)
    lane_row = lax.broadcasted_iota(jnp.int32, (1, n), 1)
    for t in range(0, GROUP, 2):
        c0 = jnp.broadcast_to(a[:, t : t + 1], (n, n))
        c1 = jnp.broadcast_to(a[:, t + 1 : t + 2], (n, n))
        p, q = c0[t : t + 1, :], c1[t : t + 1, :]
        u, s = c0[t + 1 : t + 2, :], c1[t + 1 : t + 2, :]
        inv = 1.0 / (p * s - q * u)
        here = lane_row == t
        there = lane_row == t + 1
        r0 = jnp.where(here, 1.0, jnp.where(there, 0.0, a[t : t + 1, :]))
        r1 = jnp.where(here, 0.0, jnp.where(there, 1.0, a[t + 1 : t + 2, :]))
        w0 = (s * inv) * r0 - (q * inv) * r1
        w1 = (p * inv) * r1 - (u * inv) * r0
        base = jnp.where((lane == t) | (lane == t + 1), 0.0, a)
        base = base - c0 * w0 - c1 * w1
        a = jnp.where(sub == t, w0, jnp.where(sub == t + 1, w1, base))
    a = pltpu.roll(a, n - GROUP, axis=1)
    return jnp.concatenate([a[GROUP:], a[:GROUP]], axis=0)


def scales(h):
    n = h.shape[0]
    eye = lax.broadcasted_iota(jnp.int32, (n, n), 1) == lax.broadcasted_iota(jnp.int32, (n, n), 0)
    kept = jnp.where(eye, h, 0.0)
    across = lax.rsqrt(jnp.sum(kept, axis=0, keepdims=True))
    down = lax.rsqrt(jnp.sum(kept, axis=1, keepdims=True))
    return down, across


def kernel(
    dims,
    blocks,
    t_hbm,
    a_hbm,
    c_hbm,
    gc_hbm,
    b_out,
    c_out,
    tbuf,
    part,
    mloc,
    xrecv,
    xsum,
    zrecv,
    bfull,
    ga_all,
    own,
    g1,
    g1_in,
    g2,
    g3,
    mj_all,
    mc_all,
    inv_ref,
    acc_ref,
    a_ref,
    c_ref,
    gc_ref,
    t_sem,
    x_send,
    x_recv,
    z_send,
    z_recv,
    p_send,
    p_recv,
    q_send,
    q_recv,
    ga_send,
    ga_recv,
    g1_send,
    g1_recv,
    g2_send,
    g2_recv,
    g3_send,
    g3_recv,
    mj_send,
    mj_recv,
    mc_send,
    mc_recv,
    o_sem,
    i_sem,
):
    ni, nj, nk = dims
    kl, rows, rank = part.shape
    jb = rows // blocks
    jx = jb // nk
    jz = jx // ni
    mi, mj, mk = lax.axis_index("ia"), lax.axis_index("ja"), lax.axis_index("ka")
    sends = []

    def peer(axis, me, n, d):
        return {axis: lax.rem(me + d, n)}

    def remote(src, dst, ss, rs, who):
        cp = pltpu.make_async_remote_copy(
            src_ref=src, dst_ref=dst, send_sem=ss, recv_sem=rs, device_id=who, device_id_type=MESH
        )
        cp.start()
        sends.append(cp)
        return cp

    icopies = []
    for n, (src, dst) in enumerate(((a_hbm, a_ref), (c_hbm, c_ref), (gc_hbm, gc_ref))):
        cp = pltpu.make_async_copy(src, dst, i_sem.at[n])
        cp.start()
        icopies.append(cp)
    spot = mk * nj + mj

    def side(e):
        other = lax.rem(spot + e, nk * nj)
        return {"ka": lax.div(other, nj), "ja": lax.rem(other, nj)}

    tcopies = {}
    for b in range(blocks):
        for k in range(kl):
            rs = pl.ds(b * jb, jb)
            cp = pltpu.make_async_copy(t_hbm.at[rs, k, :], tbuf.at[k, rs, :], t_sem.at[b, k])
            cp.start()
            tcopies[b, k] = cp

    barrier = pltpu.get_barrier_semaphore()
    for d in range(1, ni):
        pl.semaphore_signal(barrier, inc=1, device_id=peer("ia", mi, ni, d), device_id_type=MESH)
    for e in range(1, nk * nj):
        pl.semaphore_signal(barrier, inc=1, device_id=side(e), device_id_type=MESH)

    for cp in icopies:
        cp.wait()
    a = a_ref[...]
    a_hi = a.astype(jnp.bfloat16)
    a_lo = (a - a_hi.astype(jnp.float32)).astype(jnp.bfloat16)
    weights = jnp.concatenate([a_hi, a_lo], axis=1)
    ga_all[mi] = mtm(a)

    x_cp, z_cp, p_cp, q_cp = {}, {}, {}, {}
    step = min(256, jb)

    def first(b):
        for k in range(kl):
            tcopies[b, k].wait()

        def chunk(s, carry):
            rs = pl.ds(pl.multiple_of(b * jb + s * step, step), step)
            total = None
            for k in range(kl):
                x = tbuf[k, rs, :]
                hi = x.astype(jnp.bfloat16)
                lo = (x - hi.astype(jnp.float32)).astype(jnp.bfloat16)
                y = jnp.dot(hi, weights, preferred_element_type=jnp.float32) + jnp.dot(
                    lo, weights, preferred_element_type=jnp.float32
                )
                y = y[:, :rank] + y[:, rank:]
                part[k, rs, :] = y
                y = y * c_ref[k : k + 1, :]
                total = y if total is None else total + y
            mloc[rs, :] = total
            return carry

        lax.fori_loop(0, jb // step, chunk, 0)

    def send_first(b):
        for d in range(1, nk):
            other = lax.rem(mk + d, nk)
            rs = pl.ds(pl.multiple_of(b * jb + other * jx, 8), jx)
            x_cp[b, d] = remote(
                mloc.at[rs, :], xrecv.at[b, d - 1], x_send.at[b, d - 1], x_recv.at[b, d - 1],
                peer("ka", mk, nk, d),
            )

    def second(b):
        total = mloc[pl.ds(pl.multiple_of(b * jb + mk * jx, 8), jx), :]
        for d in range(1, nk):
            x_cp[b, d].wait_recv()
            total = total + xrecv[b, d - 1]
        xsum[b] = total
        for d in range(1, ni):
            other = lax.rem(mi + d, ni)
            z_cp[b, d] = remote(
                xsum.at[b, pl.ds(pl.multiple_of(other * jz, 8), jz), :], zrecv.at[b, d - 1],
                z_send.at[b, d - 1], z_recv.at[b, d - 1], peer("ia", mi, ni, d),
            )

    def third(b):
        total = xsum[b, pl.ds(pl.multiple_of(mi * jz, 8), jz), :]
        for d in range(1, ni):
            z_cp[b, d].wait_recv()
            total = total + zrecv[b, d - 1]
        rs = pl.ds(pl.multiple_of(b * jb + mk * jx + mi * jz, 8), jz)
        value = mm(total, inv_ref[...])
        bfull[rs, :] = value
        own[pl.ds(b * jz, jz), :] = value
        for d in range(1, ni):
            p_cp[b, d] = remote(
                bfull.at[rs, :], bfull.at[rs, :], p_send.at[b, d - 1], p_recv.at[b, d - 1],
                peer("ia", mi, ni, d),
            )

    def fourth(b):
        for d in range(1, ni):
            p_cp[b, d].wait_recv()
        rs = pl.ds(pl.multiple_of(b * jb + mk * jx, 8), jx)
        for d in range(1, nk):
            q_cp[b, d] = remote(
                bfull.at[rs, :], bfull.at[rs, :], q_send.at[b, d - 1], q_recv.at[b, d - 1],
                peer("ka", mk, nk, d),
            )

    out_cp = []

    def fifth(b):
        for d in range(1, nk):
            q_cp[b, d].wait_recv()
        rs = pl.ds(b * jb, jb)
        cp = pltpu.make_async_copy(bfull.at[rs, :], b_out.at[rs, :], o_sem.at[b])
        cp.start()
        out_cp.append(cp)
        value = bfull[rs, :]
        for k in range(kl):
            s = jnp.sum(part[k, rs, :] * value, axis=0, keepdims=True)
            acc_ref[pl.ds(k, 1), :] = acc_ref[pl.ds(k, 1), :] + s

    first(0)
    pl.semaphore_wait(barrier, ni + nk * nj - 2)
    ga_cp = [
        remote(ga_all.at[mi], ga_all.at[mi], ga_send.at[d - 1], ga_recv.at[d - 1], peer("ia", mi, ni, d))
        for d in range(1, ni)
    ]
    send_first(0)
    for b in range(1, blocks):
        first(b)
        send_first(b)

    acc_ref[...] = jnp.zeros_like(acc_ref)
    for cp in ga_cp:
        cp.wait_recv()
    gram_a = ga_all[0]
    for d in range(1, ni):
        gram_a = gram_a + ga_all[d]
    groups = rank // GROUP

    def turn(h, quarter):
        lo, hi = groups * quarter // 4, groups * (quarter + 1) // 4
        return lax.fori_loop(lo, hi, lambda _, v: eliminate(v), h)

    h = gram_a * gc_ref[...]
    down, across = scales(h)
    h = h * down * across
    at = 0
    for quarter in range(4):
        h = turn(h, quarter)
        while at < blocks * (quarter + 1) // 4:
            second(at)
            at += 1
    inv_ref[...] = h * down * across
    for b in range(blocks):
        third(b)
        if b >= 1:
            fourth(b - 1)

    cut = rank // ni if rank % (8 * ni) == 0 else rank
    split = cut != rank
    g1[...] = mtm(own[...])
    mine = pl.ds(pl.multiple_of(mi * cut, 8), cut) if split else pl.ds(0, rank)
    g1_in[mi] = g1[mine, :]
    g1_cp = []
    for d in range(1, ni):
        other = lax.rem(mi + d, ni)
        rs = pl.ds(pl.multiple_of(other * cut, 8), cut) if split else pl.ds(0, rank)
        g1_cp.append(
            remote(g1.at[rs, :], g1_in.at[mi], g1_send.at[d - 1], g1_recv.at[d - 1], peer("ia", mi, ni, d))
        )
    fourth(blocks - 1)
    for cp in g1_cp:
        cp.wait_recv()
    total = g1_in[0]
    for d in range(1, ni):
        total = total + g1_in[d]
    g2[spot] = total
    g2_cp = [
        remote(g2.at[spot], g2.at[spot], g2_send.at[e - 1], g2_recv.at[e - 1], side(e))
        for e in range(1, nk * nj)
    ]
    half = blocks // 2
    for b in range(half):
        fifth(b)
    for cp in g2_cp:
        cp.wait_recv()
    total = g2[0]
    for e in range(1, nk * nj):
        total = total + g2[e]
    g3[mine, :] = total
    g3_cp = []
    if split:
        g3_cp = [
            remote(g3.at[mine, :], g3.at[mine, :], g3_send.at[d - 1], g3_recv.at[d - 1], peer("ia", mi, ni, d))
            for d in range(1, ni)
        ]
    for b in range(half, blocks - 1):
        fifth(b)
    for cp in g3_cp:
        cp.wait_recv()
    h = gram_a * g3[...]
    down, across = scales(h)
    h = turn(h * down * across, 0)
    fifth(blocks - 1)
    mj_all[mj] = acc_ref[...]
    mj_cp = [
        remote(mj_all.at[mj], mj_all.at[mj], mj_send.at[d - 1], mj_recv.at[d - 1], peer("ja", mj, nj, d))
        for d in range(1, nj)
    ]
    h = turn(h, 1)
    for cp in mj_cp:
        cp.wait_recv()
    total = mj_all[0]
    for d in range(1, nj):
        total = total + mj_all[d]
    mc_all[mi] = total
    mc_cp = [
        remote(mc_all.at[mi], mc_all.at[mi], mc_send.at[d - 1], mc_recv.at[d - 1], peer("ia", mi, ni, d))
        for d in range(1, ni)
    ]
    h = turn(turn(h, 2), 3)
    inverse = h * down * across
    for cp in mc_cp:
        cp.wait_recv()
    mttkrp_c = mc_all[0]
    for d in range(1, ni):
        mttkrp_c = mttkrp_c + mc_all[d]
    c_out[...] = mm(mttkrp_c, inverse)[:kl, :]
    for cp in out_cp:
        cp.wait()
    for cp in sends:
        cp.wait_send()


def body(dims, tensor, factor_a, factor_c, gram_c):
    ni, nj, nk = dims
    rows, kl, il = tensor.shape
    rank = factor_a.shape[1]
    blocks = 4
    jb = rows // blocks
    jx = jb // nk
    jz = jx // ni
    kp = -(-kl // 8) * 8
    cut = rank // ni if rank % (8 * ni) == 0 else rank
    f32 = jnp.float32
    dma = pltpu.SemaphoreType.DMA
    vmem = pl.BlockSpec(memory_space=pltpu.VMEM)
    return pl.pallas_call(
        functools.partial(kernel, dims, blocks),
        out_shape=(
            jax.ShapeDtypeStruct((rows, rank), f32),
            jax.ShapeDtypeStruct((kl, rank), f32),
        ),
        in_specs=[pl.BlockSpec(memory_space=pltpu.HBM)] * 4,
        out_specs=(pl.BlockSpec(memory_space=pl.ANY), vmem),
        scratch_shapes=[
            pltpu.VMEM((kl, rows, il), f32),
            pltpu.VMEM((kl, rows, rank), f32),
            pltpu.VMEM((rows, rank), f32),
            pltpu.VMEM((blocks, nk - 1, jx, rank), f32),
            pltpu.VMEM((blocks, jx, rank), f32),
            pltpu.VMEM((blocks, ni - 1, jz, rank), f32),
            pltpu.VMEM((rows, rank), f32),
            pltpu.VMEM((ni, rank, rank), f32),
            pltpu.VMEM((blocks * jz, rank), f32),
            pltpu.VMEM((rank, rank), f32),
            pltpu.VMEM((ni, cut, rank), f32),
            pltpu.VMEM((nk * nj, cut, rank), f32),
            pltpu.VMEM((rank, rank), f32),
            pltpu.VMEM((nj, kp, rank), f32),
            pltpu.VMEM((ni, kp, rank), f32),
            pltpu.VMEM((rank, rank), f32),
            pltpu.VMEM((kp, rank), f32),
            pltpu.VMEM((il, rank), f32),
            pltpu.VMEM((kl, rank), f32),
            pltpu.VMEM((rank, rank), f32),
            dma((blocks, kl)),
            dma((blocks, nk - 1)),
            dma((blocks, nk - 1)),
            dma((blocks, ni - 1)),
            dma((blocks, ni - 1)),
            dma((blocks, ni - 1)),
            dma((blocks, ni - 1)),
            dma((blocks, nk - 1)),
            dma((blocks, nk - 1)),
            dma((ni - 1,)),
            dma((ni - 1,)),
            dma((ni - 1,)),
            dma((ni - 1,)),
            dma((nk * nj - 1,)),
            dma((nk * nj - 1,)),
            dma((ni - 1,)),
            dma((ni - 1,)),
            dma((nj - 1,)),
            dma((nj - 1,)),
            dma((ni - 1,)),
            dma((ni - 1,)),
            dma((blocks,)),
            dma((3,)),
        ],
        compiler_params=pltpu.CompilerParams(
            collective_id=0, has_side_effects=True, vmem_limit_bytes=48 * 1024 * 1024
        ),
    )(tensor, factor_a, factor_c, gram_c)


def solution(mesh):
    dims = (mesh.shape["ia"], mesh.shape["ja"], mesh.shape["ka"])
    placed = (P("ja", "ka", "ia"), P("ia", None), P("ka", None), P())
    return jax.shard_map(
        functools.partial(body, dims),
        mesh=mesh,
        in_specs=placed,
        out_specs=(P("ja", None), P("ka", None)),
        check_vma=False,
    )
```

```python
import functools

import jax
import jax.numpy as jnp
from jax import lax
from jax.experimental import pallas as pl
from jax.experimental.pallas import tpu as pltpu
from jax.sharding import PartitionSpec as P

HIGH = lax.Precision.HIGHEST
MESH = pl.DeviceIdType.MESH
GROUP = 16


def mm(a, b):
    return jnp.dot(a, b, precision=HIGH, preferred_element_type=jnp.float32)


def mtm(a):
    return lax.dot_general(
        a, a, (((0,), (0,)), ((), ())), precision=HIGH, preferred_element_type=jnp.float32
    )


def eliminate(a):
    n = a.shape[0]
    lane = lax.broadcasted_iota(jnp.int32, (n, n), 1)
    sub = lax.broadcasted_iota(jnp.int32, (n, n), 0)
    lane_row = lax.broadcasted_iota(jnp.int32, (1, n), 1)
    for t in range(0, GROUP, 2):
        c0 = jnp.broadcast_to(a[:, t : t + 1], (n, n))
        c1 = jnp.broadcast_to(a[:, t + 1 : t + 2], (n, n))
        p, q = c0[t : t + 1, :], c1[t : t + 1, :]
        u, s = c0[t + 1 : t + 2, :], c1[t + 1 : t + 2, :]
        inv = 1.0 / (p * s - q * u)
        here = lane_row == t
        there = lane_row == t + 1
        r0 = jnp.where(here, 1.0, jnp.where(there, 0.0, a[t : t + 1, :]))
        r1 = jnp.where(here, 0.0, jnp.where(there, 1.0, a[t + 1 : t + 2, :]))
        w0 = (s * inv) * r0 - (q * inv) * r1
        w1 = (p * inv) * r1 - (u * inv) * r0
        base = jnp.where((lane == t) | (lane == t + 1), 0.0, a)
        base = base - c0 * w0 - c1 * w1
        a = jnp.where(sub == t, w0, jnp.where(sub == t + 1, w1, base))
    a = pltpu.roll(a, n - GROUP, axis=1)
    return jnp.concatenate([a[GROUP:], a[:GROUP]], axis=0)


def scales(h):
    n = h.shape[0]
    eye = lax.broadcasted_iota(jnp.int32, (n, n), 1) == lax.broadcasted_iota(jnp.int32, (n, n), 0)
    kept = jnp.where(eye, h, 0.0)
    across = lax.rsqrt(jnp.sum(kept, axis=0, keepdims=True))
    down = lax.rsqrt(jnp.sum(kept, axis=1, keepdims=True))
    return down, across


def kernel(
    dims,
    blocks,
    t_hbm,
    a_hbm,
    c_hbm,
    gc_hbm,
    b_out,
    c_out,
    tbuf,
    part,
    mloc,
    xrecv,
    xsum,
    zrecv,
    bfull,
    ga_loc,
    ga_in,
    ga_full,
    g1,
    g1_in,
    g3,
    mj_all,
    mc_all,
    inv_ref,
    acc_ref,
    a_ref,
    c_ref,
    gc_ref,
    t_sem,
    x_send,
    x_recv,
    z_send,
    z_recv,
    p_send,
    p_recv,
    q_send,
    q_recv,
    ga_send,
    ga_recv,
    gf_send,
    gf_recv,
    g1_send,
    g1_recv,
    g3_send,
    g3_recv,
    mj_send,
    mj_recv,
    mc_send,
    mc_recv,
    o_sem,
    i_sem,
):
    ni, nj, nk = dims
    kl, rows, rank = part.shape
    jb = rows // blocks
    jx = jb // nk
    jz = jx // ni
    mi, mj, mk = lax.axis_index("ia"), lax.axis_index("ja"), lax.axis_index("ka")
    sends = []

    def peer(axis, me, n, d):
        return {axis: lax.rem(me + d, n)}

    def remote(src, dst, ss, rs, who):
        cp = pltpu.make_async_remote_copy(
            src_ref=src, dst_ref=dst, send_sem=ss, recv_sem=rs, device_id=who, device_id_type=MESH
        )
        cp.start()
        sends.append(cp)
        return cp

    icopies = []
    for n, (src, dst) in enumerate(((a_hbm, a_ref), (c_hbm, c_ref), (gc_hbm, gc_ref))):
        cp = pltpu.make_async_copy(src, dst, i_sem.at[n])
        cp.start()
        icopies.append(cp)
    tcopies = {}
    for b in range(blocks):
        for k in range(kl):
            rs = pl.ds(b * jb, jb)
            cp = pltpu.make_async_copy(t_hbm.at[rs, k, :], tbuf.at[k, rs, :], t_sem.at[b, k])
            cp.start()
            tcopies[b, k] = cp

    barrier = pltpu.get_barrier_semaphore()
    for d in range(1, ni):
        pl.semaphore_signal(barrier, inc=1, device_id=peer("ia", mi, ni, d), device_id_type=MESH)
    for d in range(1, nj):
        pl.semaphore_signal(barrier, inc=1, device_id=peer("ja", mj, nj, d), device_id_type=MESH)
    for d in range(1, nk):
        pl.semaphore_signal(barrier, inc=1, device_id=peer("ka", mk, nk, d), device_id_type=MESH)

    for cp in icopies:
        cp.wait()
    a = a_ref[...]
    a_hi = a.astype(jnp.bfloat16)
    a_lo = (a - a_hi.astype(jnp.float32)).astype(jnp.bfloat16)
    weights = jnp.concatenate([a_hi, a_lo], axis=1)
    ga_loc[...] = mtm(a)

    x_cp, z_cp, p_cp, q_cp = {}, {}, {}, {}
    step = min(256, jb)

    def first(b):
        for k in range(kl):
            tcopies[b, k].wait()

        def chunk(s, carry):
            rs = pl.ds(pl.multiple_of(b * jb + s * step, step), step)
            total = None
            for k in range(kl):
                x = tbuf[k, rs, :]
                hi = x.astype(jnp.bfloat16)
                lo = (x - hi.astype(jnp.float32)).astype(jnp.bfloat16)
                y = jnp.dot(hi, weights, preferred_element_type=jnp.float32) + jnp.dot(
                    lo, weights, preferred_element_type=jnp.float32
                )
                y = y[:, :rank] + y[:, rank:]
                part[k, rs, :] = y
                y = y * c_ref[k : k + 1, :]
                total = y if total is None else total + y
            mloc[rs, :] = total
            return carry

        lax.fori_loop(0, jb // step, chunk, 0)

    def send_first(b):
        for d in range(1, nk):
            other = lax.rem(mk + d, nk)
            rs = pl.ds(pl.multiple_of(b * jb + other * jx, 8), jx)
            x_cp[b, d] = remote(
                mloc.at[rs, :], xrecv.at[b, d - 1], x_send.at[b, d - 1], x_recv.at[b, d - 1],
                peer("ka", mk, nk, d),
            )

    hops = []
    while 2 ** len(hops) < ni:
        hops.append(2 ** len(hops))
    levels = len(hops)
    bits = [lax.rem(lax.div(mi, m), 2) for m in hops]
    starts, arrive = [0], [0]
    for n in range(levels):
        starts.append(starts[n] + bits[n] * (jx >> (n + 1)))
        arrive.append(arrive[n] + (jx >> (n + 1)))

    def across_ia(n):
        return {"ia": mi + hops[n] * (1 - 2 * bits[n])}

    def z_start(b, n):
        size = jx >> (n + 1)
        give = pl.ds(pl.multiple_of(starts[n] + (1 - bits[n]) * size, 8), size)
        z_cp[b, n] = remote(
            xsum.at[b, give, :], zrecv.at[b, pl.ds(arrive[n], size), :], z_send.at[b, n],
            z_recv.at[b, n], across_ia(n),
        )

    def z_finish(b, n):
        size = jx >> (n + 1)
        z_cp[b, n].wait_recv()
        keep = pl.ds(pl.multiple_of(starts[n + 1], 8), size)
        return keep, xsum[b, keep, :] + zrecv[b, pl.ds(arrive[n], size), :]

    def p_start(b, n):
        rs = pl.ds(pl.multiple_of(b * jb + mk * jx + starts[n + 1], 8), jx >> (n + 1))
        p_cp[b, n] = remote(
            bfull.at[rs, :], bfull.at[rs, :], p_send.at[b, n], p_recv.at[b, n], across_ia(n)
        )

    def second(b):
        total = mloc[pl.ds(pl.multiple_of(b * jb + mk * jx, 8), jx), :]
        for d in range(1, nk):
            x_cp[b, d].wait_recv()
            total = total + xrecv[b, d - 1]
        xsum[b] = total
        z_start(b, 0)

    def reduce_more(b):
        for n in range(levels - 1):
            keep, value = z_finish(b, n)
            xsum[b, keep, :] = value
            z_start(b, n + 1)

    def third(b):
        _, total = z_finish(b, levels - 1)
        rs = pl.ds(pl.multiple_of(b * jb + mk * jx + starts[levels], 8), jz)
        bfull[rs, :] = mm(total, inv_ref[...])
        p_start(b, levels - 1)

    def gather_more(b):
        for n in range(levels - 1, 0, -1):
            p_cp[b, n].wait_recv()
            p_start(b, n - 1)

    def fourth(b):
        p_cp[b, 0].wait_recv()
        rs = pl.ds(pl.multiple_of(b * jb + mk * jx, 8), jx)
        for d in range(1, nk):
            q_cp[b, d] = remote(
                bfull.at[rs, :], bfull.at[rs, :], q_send.at[b, d - 1], q_recv.at[b, d - 1],
                peer("ka", mk, nk, d),
            )

    out_cp = []

    def fifth(b):
        for d in range(1, nk):
            q_cp[b, d].wait_recv()
        rs = pl.ds(b * jb, jb)
        cp = pltpu.make_async_copy(bfull.at[rs, :], b_out.at[rs, :], o_sem.at[b])
        cp.start()
        out_cp.append(cp)
        value = bfull[rs, :]
        g1[...] = g1[...] + mtm(value)
        for k in range(kl):
            s = jnp.sum(part[k, rs, :] * value, axis=0, keepdims=True)
            acc_ref[pl.ds(k, 1), :] = acc_ref[pl.ds(k, 1), :] + s

    first(0)
    pl.semaphore_wait(barrier, ni + nj + nk - 3)
    strip = rank // nj
    part_rows = pl.ds(pl.multiple_of(mj * strip, 8), strip)
    ga_in[mi] = ga_loc[part_rows, :]
    ga_cp = [
        remote(
            ga_loc.at[part_rows, :], ga_in.at[mi], ga_send.at[d - 1], ga_recv.at[d - 1],
            peer("ia", mi, ni, d),
        )
        for d in range(1, ni)
    ]
    send_first(0)
    gf_cp = []
    for b in range(1, blocks):
        first(b)
        send_first(b)
        if b == min(2, blocks - 1):
            for cp in ga_cp:
                cp.wait_recv()
            total = ga_in[0]
            for d in range(1, ni):
                total = total + ga_in[d]
            ga_full[part_rows, :] = total
            for d in range(1, nj):
                gf_cp.append(
                    remote(
                        ga_full.at[part_rows, :], ga_full.at[part_rows, :], gf_send.at[d - 1],
                        gf_recv.at[d - 1], peer("ja", mj, nj, d),
                    )
                )

    acc_ref[...] = jnp.zeros_like(acc_ref)
    g1[...] = jnp.zeros_like(g1)
    second(0)
    for cp in gf_cp:
        cp.wait_recv()
    gram_a = ga_full[...]
    groups = rank // GROUP

    def turn(h, quarter):
        lo, hi = groups * quarter // 4, groups * (quarter + 1) // 4
        return lax.fori_loop(lo, hi, lambda _, v: eliminate(v), h)

    h = gram_a * gc_ref[...]
    down, across = scales(h)
    h = h * down * across
    h = turn(turn(h, 0), 1)
    second(1)
    reduce_more(0)
    h = turn(turn(h, 2), 3)
    inv_ref[...] = h * down * across
    stages = (second, reduce_more, third, gather_more, fourth, fifth)
    done = [2, 1, 0, 0, 0, 0]
    while done[5] < blocks:
        for n in range(6):
            if done[n] < (blocks if n == 0 else before[n - 1]):
                stages[n](done[n])
                done[n] += 1
            if n == 0:
                before = list(done)

    cut = rank // nj
    mine = pl.ds(pl.multiple_of(mj * cut, 8), cut)
    g1_in[mj] = g1[mine, :]
    g1_cp = []
    for d in range(1, nj):
        rs = pl.ds(pl.multiple_of(lax.rem(mj + d, nj) * cut, 8), cut)
        g1_cp.append(
            remote(g1.at[rs, :], g1_in.at[mj], g1_send.at[d - 1], g1_recv.at[d - 1], peer("ja", mj, nj, d))
        )
    mj_all[mj] = acc_ref[...]
    mj_cp = [
        remote(mj_all.at[mj], mj_all.at[mj], mj_send.at[d - 1], mj_recv.at[d - 1], peer("ja", mj, nj, d))
        for d in range(1, nj)
    ]
    for cp in g1_cp:
        cp.wait_recv()
    total = g1_in[0]
    for d in range(1, nj):
        total = total + g1_in[d]
    g3[mine, :] = total
    g3_cp = [
        remote(g3.at[mine, :], g3.at[mine, :], g3_send.at[d - 1], g3_recv.at[d - 1], peer("ja", mj, nj, d))
        for d in range(1, nj)
    ]
    for cp in mj_cp:
        cp.wait_recv()
    total = mj_all[0]
    for d in range(1, nj):
        total = total + mj_all[d]
    mc_all[mi] = total
    mc_cp = [
        remote(mc_all.at[mi], mc_all.at[mi], mc_send.at[d - 1], mc_recv.at[d - 1], peer("ia", mi, ni, d))
        for d in range(1, ni)
    ]
    for cp in g3_cp:
        cp.wait_recv()
    h = gram_a * g3[...]
    down, across = scales(h)
    h = h * down * across
    for quarter in range(4):
        h = turn(h, quarter)
    inverse = h * down * across
    for cp in mc_cp:
        cp.wait_recv()
    mttkrp_c = mc_all[0]
    for d in range(1, ni):
        mttkrp_c = mttkrp_c + mc_all[d]
    c_out[...] = mm(mttkrp_c, inverse)[:kl, :]
    for cp in out_cp:
        cp.wait()
    for cp in sends:
        cp.wait_send()


def body(dims, tensor, factor_a, factor_c, gram_c):
    ni, nj, nk = dims
    rows, kl, il = tensor.shape
    rank = factor_a.shape[1]
    blocks = 4
    jb = rows // blocks
    jx = jb // nk
    jz = jx // ni
    kp = -(-kl // 8) * 8
    hops = (ni - 1).bit_length()
    strip = rank // nj
    f32 = jnp.float32
    dma = pltpu.SemaphoreType.DMA
    vmem = pl.BlockSpec(memory_space=pltpu.VMEM)
    return pl.pallas_call(
        functools.partial(kernel, dims, blocks),
        out_shape=(
            jax.ShapeDtypeStruct((rows, rank), f32),
            jax.ShapeDtypeStruct((kl, rank), f32),
        ),
        in_specs=[pl.BlockSpec(memory_space=pltpu.HBM)] * 4,
        out_specs=(pl.BlockSpec(memory_space=pl.ANY), vmem),
        scratch_shapes=[
            pltpu.VMEM((kl, rows, il), f32),
            pltpu.VMEM((kl, rows, rank), f32),
            pltpu.VMEM((rows, rank), f32),
            pltpu.VMEM((blocks, nk - 1, jx, rank), f32),
            pltpu.VMEM((blocks, jx, rank), f32),
            pltpu.VMEM((blocks, jx, rank), f32),
            pltpu.VMEM((rows, rank), f32),
            pltpu.VMEM((rank, rank), f32),
            pltpu.VMEM((ni, strip, rank), f32),
            pltpu.VMEM((rank, rank), f32),
            pltpu.VMEM((rank, rank), f32),
            pltpu.VMEM((nj, rank // nj, rank), f32),
            pltpu.VMEM((rank, rank), f32),
            pltpu.VMEM((nj, kp, rank), f32),
            pltpu.VMEM((ni, kp, rank), f32),
            pltpu.VMEM((rank, rank), f32),
            pltpu.VMEM((kp, rank), f32),
            pltpu.VMEM((il, rank), f32),
            pltpu.VMEM((kl, rank), f32),
            pltpu.VMEM((rank, rank), f32),
            dma((blocks, kl)),
            dma((blocks, nk - 1)),
            dma((blocks, nk - 1)),
            dma((blocks, hops)),
            dma((blocks, hops)),
            dma((blocks, hops)),
            dma((blocks, hops)),
            dma((blocks, nk - 1)),
            dma((blocks, nk - 1)),
            dma((ni - 1,)),
            dma((ni - 1,)),
            dma((nj - 1,)),
            dma((nj - 1,)),
            dma((nj - 1,)),
            dma((nj - 1,)),
            dma((nj - 1,)),
            dma((nj - 1,)),
            dma((nj - 1,)),
            dma((nj - 1,)),
            dma((ni - 1,)),
            dma((ni - 1,)),
            dma((blocks,)),
            dma((3,)),
        ],
        compiler_params=pltpu.CompilerParams(
            collective_id=0, has_side_effects=True, vmem_limit_bytes=48 * 1024 * 1024
        ),
    )(tensor, factor_a, factor_c, gram_c)


def solution(mesh):
    dims = (mesh.shape["ia"], mesh.shape["ja"], mesh.shape["ka"])
    placed = (P("ja", "ka", "ia"), P("ia", None), P("ka", None), P())
    return jax.shard_map(
        functools.partial(body, dims),
        mesh=mesh,
        in_specs=placed,
        out_specs=(P("ja", None), P("ka", None)),
        check_vma=False,
    )
```
